512 devices in a mesh: row: 8 (over z_hi, core), col: 16 (over x, y), fsdp: 4 (over z_lo).
Axes of the slice: x: 4, y: 4, z: 16 (z_hi: 4, z_lo: 4; z = z_hi * 4 + z_lo), core: 2. Of those that a mesh axis runs over, the one named last changes fastest.
Arguments:
- layer_inputs: bfloat16 [4096, 8192], P('col', ('row', 'fsdp')), may hold values from -6 to 6
- output_grads: bfloat16 [4096, 14336], P(('row', 'fsdp'), 'col'), may hold values from -0.09375 to 0.09375
- weight: bfloat16 [8192, 14336], P(('row', 'fsdp'), 'col'), may hold values from -3 to 3
- moment: bfloat16 [8192, 14336], P(('row', 'fsdp'), 'col'), may hold values from -1.796875 to 1.796875
- variance: bfloat16 [8192, 14336], P(('row', 'fsdp'), 'col'), may hold values from 0.049804688 to 1
- keep_mask: int32 [64, 112], replicated, may hold values from 0 to 1, as said below
Outputs:
- new_weight: bfloat16 [8192, 14336], P(('row', 'fsdp'), 'col')
- new_moment: bfloat16 [8192, 14336], P(('row', 'fsdp'), 'col')
- new_variance: bfloat16 [8192, 14336], P(('row', 'fsdp'), 'col')
The draws below stay inside these ranges and needn't reach their ends.
Inputs may be any that keep to these rules, and one draw needn't show every extreme that they name: `keep_mask`: 1 keeps a block of 128 x 128 weights, 0 drops it.
All inputs are finite; a program needn't handle non-finite values.
Results may differ from the reference program's by a relative error of at most 0.0039.
Values may be sent and summed in bfloat16 or wider, within the bound.
A program may use at most 128 MiB of HBM per device.

```python
import math
import jax
import jax.numpy as jnp

BS = 128
D = 8192
FF = 14336
TOKENS = 4096
KBR = 64
KBC = 112


def draw_keep_mask(key, part):
    first_key, second_key, third_key = jax.random.split(jax.random.fold_in(key, 17), 3)
    row_level = jax.random.randint(first_key, (KBR, 1), 0, 41)
    col_level = jax.random.randint(second_key, (1, KBC), 0, 41)
    scores = jax.random.randint(third_key, (KBR, KBC), 0, 100)
    return (scores < row_level + col_level).astype(jnp.int32)


def steps_of(key, shape, pieces, least, top_value):
    level, own = 1.0, jax.random.fold_in(key, 6)
    for position, blocks in pieces:
        steps = jnp.exp(jax.random.uniform(jax.random.fold_in(own, position), (blocks,), jnp.float32, least / len(pieces), top_value / len(pieces)))
        level = level * jnp.repeat(steps, shape[position] // blocks).reshape([-1 if axis == position else 1 for axis in range(len(shape))])
    return level


def normal_values(key, shape, spread, reach, pieces=(), held_as=jnp.bfloat16):
    entries = jax.random.normal(key, shape, jnp.float32) * spread
    if len(pieces) > 0:
        entries = steps_of(key, shape, pieces, -0.22, 0.18) * entries
    return jnp.clip(entries, min=-reach, max=reach).astype(held_as)


def setup_inputs(seed: int = 0) -> dict:
    streams_of = jax.random.split(jax.random.key(seed), 7)
    return {
        "layer_inputs": normal_values(streams_of[0], (TOKENS, D), 1.0, 6.0, ((0, 16), (1, 32))),
        "output_grads": normal_values(streams_of[1], (TOKENS, FF), TOKENS ** -0.5, 0.09375, ((0, 32), (1, 16))),
        "weight": normal_values(streams_of[2], (D, FF), 0.5, 3.0, ((0, 32), (1, 16))),
        "moment": normal_values(streams_of[3], (D, FF), 0.3, 1.796875, ((0, 32), (1, 16))),
        "variance": jnp.clip(jnp.exp(math.log(1.0) - 2.9996462 * jax.random.uniform(streams_of[4], (D, FF), jnp.float32) ** steps_of(streams_of[4], (D, FF), ((0, 32), (1, 16)), -0.2, 0.2)), 0.049804688, 1.0).astype(jnp.bfloat16),
        "keep_mask": draw_keep_mask(jax.random.fold_in(streams_of[6], 71), 0),
    }


learn_rate = 0.02
beta_one = 0.9
beta_two = 0.95
epsilon = 1e-08
decay_rate = 0.1
first_fix = 1.0 - 0.9 ** 10
second_fix = 1.0 - 0.95 ** 10

def expand_keep(keep_tile):
    block_rows, block_cols = keep_tile.shape
    grid = jnp.broadcast_to(keep_tile[:, None, :, None], (block_rows, BS, block_cols, BS))
    return grid.reshape(block_rows * BS, block_cols * BS) > 0

def adam_update(grad, weight, moment, variance, keep_elem):
    weight_wide = weight.astype(jnp.float32)
    first = beta_one * moment.astype(jnp.float32) + (1.0 - beta_one) * grad
    second = beta_two * variance.astype(jnp.float32) + (1.0 - beta_two) * grad * grad
    direction = first / first_fix / (jnp.sqrt(second / second_fix) + epsilon) + decay_rate * weight_wide
    new_weight = jnp.where(keep_elem, (weight_wide - learn_rate * direction).astype(jnp.bfloat16), weight)
    new_moment = jnp.where(keep_elem, first.astype(jnp.bfloat16), moment)
    new_variance = jnp.where(keep_elem, second.astype(jnp.bfloat16), variance)
    return (new_weight, new_moment, new_variance)

def reference(layer_inputs, output_grads, weight, moment, variance, keep_mask):
    grad = jnp.dot(layer_inputs.T, output_grads, preferred_element_type=jnp.float32)
    keep_elem = expand_keep(keep_mask)
    return adam_update(grad, weight, moment, variance, keep_elem)
```

```python
import jax
import jax.numpy as jnp
from jax import lax
from jax.experimental import pallas as pl
from jax.experimental.pallas import tpu as pltpu
from jax.sharding import PartitionSpec as P

BS = 128
MESH = pl.DeviceIdType.MESH

learn_rate = 0.02
beta_one = 0.9
beta_two = 0.95
epsilon = 1e-08
decay_rate = 0.1
first_fix = 1.0 - 0.9**10
second_fix = 1.0 - 0.95**10

SIDE = 4
RING = 16
FAR = RING // 2
LOW = 4
PARTS = 2
OFFSETS = (0, 3, 1, 2)


def expand_keep(keep_tile):
    block_rows, block_cols = keep_tile.shape
    grid = jnp.broadcast_to(keep_tile[:, None, :, None], (block_rows, BS, block_cols, BS))
    return grid.reshape(block_rows * BS, block_cols * BS) > 0


def adam_update(grad, weight, moment, variance, keep_elem):
    weight_wide = weight.astype(jnp.float32)
    first = beta_one * moment.astype(jnp.float32) + (1.0 - beta_one) * grad
    second = beta_two * variance.astype(jnp.float32) + (1.0 - beta_two) * grad * grad
    direction = (
        first / first_fix / (jnp.sqrt(second / second_fix) + epsilon) + decay_rate * weight_wide
    )
    new_weight = jnp.where(
        keep_elem, (weight_wide - learn_rate * direction).astype(jnp.bfloat16), weight
    )
    new_moment = jnp.where(keep_elem, first.astype(jnp.bfloat16), moment)
    new_variance = jnp.where(keep_elem, second.astype(jnp.bfloat16), variance)
    return (new_weight, new_moment, new_variance)


def grad_kernel(
    x_ref,
    g_ref,
    out_ref,
    x_all,
    g_all,
    ring_send,
    ring_recv,
    core_send,
    core_recv,
    first_send,
    first_recv,
    hop_send,
    hop_recv,
    second_send,
    second_recv,
    last_send,
    last_recv,
    local_sem,
):
    row = lax.axis_index("row")
    col = lax.axis_index("col")
    low = lax.axis_index("fsdp")
    core = lax.rem(row, 2)
    z = lax.div(row, 2) * LOW + low
    place = (lax.div(col, SIDE), lax.rem(col, SIDE))

    def row_at(level, which):
        return lax.div(level, LOW) * 2 + which

    def slot_at(level, which):
        return row_at(level, which) * LOW + lax.rem(level, LOW)

    def z_device(step):
        level = lax.rem(z + step + RING, RING)
        return {"row": row_at(level, core), "fsdp": lax.rem(level, LOW)}

    def col_at(axis, along, across):
        moved = lax.rem(place[axis] + along + SIDE, SIDE)
        other = lax.rem(place[1 - axis] + across + SIDE, SIDE)
        return moved * SIDE + other if axis == 0 else other * SIDE + moved

    def xy_device(axis, step):
        return {"col": col_at(axis, step, 0)}

    twin = {"row": row + 1 - 2 * core}
    ways = (1, -1)

    neighbours = [z_device(1), z_device(-1), twin]
    neighbours += [xy_device(axis, way) for axis in (0, 1) for way in ways]
    barrier = pltpu.get_barrier_semaphore()
    for device in neighbours:
        pl.semaphore_signal(barrier, inc=1, device_id=device, device_id_type=MESH)
    pl.semaphore_wait(barrier, len(neighbours))

    sent = []

    def send(src, dst, send_sem, recv_sem, device):
        copy = pltpu.make_async_remote_copy(
            src_ref=src,
            dst_ref=dst,
            send_sem=send_sem,
            recv_sem=recv_sem,
            device_id=device,
            device_id_type=MESH,
        )
        copy.start()
        sent.append(copy)

    def arrived(dst, send_sem, recv_sem, device):
        pltpu.make_async_remote_copy(
            src_ref=dst,
            dst_ref=dst,
            send_sem=send_sem,
            recv_sem=recv_sem,
            device_id=device,
            device_id_type=MESH,
        ).wait_recv()

    tokens = g_ref.shape[0]
    piece = tokens // PARTS

    def part(k):
        return pl.ds(k * piece, piece)

    def goes(step, d, k):
        return step < FAR or (step == FAR and (k < PARTS // 2) == (d == 0))

    def ring_start(step, d, k, src, slot):
        send(
            src,
            g_all.at[slot, part(k), :],
            ring_send.at[d, step - 1, k],
            ring_recv.at[d, step - 1, k],
            z_device(ways[d]),
        )

    def ring_step(step):
        for k in range(PARTS):
            for d in (0, 1):
                if not goes(step, d, k):
                    continue
                slot = slot_at(lax.rem(z - ways[d] * step + RING, RING), core)
                here = g_all.at[slot, part(k), :]
                sems = (ring_send.at[d, step - 1, k], ring_recv.at[d, step - 1, k])
                arrived(here, *sems, z_device(ways[d]))
                if goes(step + 1, d, k):
                    ring_start(step + 1, d, k, here, slot)
                send(here, here, core_send.at[d, step - 1, k], core_recv.at[d, step - 1, k], twin)

    def core_step(step):
        for k in range(PARTS):
            for d in (0, 1):
                if not goes(step, d, k):
                    continue
                slot = slot_at(lax.rem(z - ways[d] * step + RING, RING), 1 - core)
                arrived(
                    g_all.at[slot, part(k), :],
                    core_send.at[d, step - 1, k],
                    core_recv.at[d, step - 1, k],
                    twin,
                )

    half = x_ref.shape[0] // 2
    quarter = half // 2

    def half_of(h):
        return pl.ds(h * half, half)

    def quarter_of(h, d):
        return pl.ds(h * half + d * quarter, quarter)

    def along_first(h, d):
        src = x_ref.at[half_of(h), :]
        dst = x_all.at[col, half_of(h), :]
        send(src, dst, first_send.at[h, d], first_recv.at[h, d], xy_device(h, ways[d]))

    def along_second(h, o):
        slot = col_at(h, OFFSETS[o], 0)
        here = x_all.at[slot, half_of(h), :]
        src = x_ref.at[half_of(h), :] if o == 0 else here
        for d in (0, 1):
            send(src, here, second_send.at[h, o, d], second_recv.at[h, o, d], xy_device(1 - h, ways[d]))

    def first_in(h, d):
        slot = col_at(h, -ways[d], 0)
        arrived(x_all.at[slot, half_of(h), :], first_send.at[h, d], first_recv.at[h, d], xy_device(h, ways[d]))
        on = x_all.at[slot, quarter_of(h, d), :]
        send(on, on, hop_send.at[h, d], hop_recv.at[h, d], xy_device(h, ways[d]))
        along_second(h, 1 + d)

    def hop_in(h):
        slot = col_at(h, 2, 0)
        for d in (0, 1):
            on = x_all.at[slot, quarter_of(h, d), :]
            arrived(on, hop_send.at[h, d], hop_recv.at[h, d], xy_device(h, ways[d]))
        along_second(h, 3)

    def second_in(h, o):
        for d in (0, 1):
            slot = col_at(h, OFFSETS[o], -ways[d])
            sems = (second_send.at[h, o, d], second_recv.at[h, o, d])
            arrived(x_all.at[slot, half_of(h), :], *sems, xy_device(1 - h, ways[d]))
            on = x_all.at[slot, quarter_of(h, d), :]
            send(on, on, last_send.at[h, o, d], last_recv.at[h, o, d], xy_device(1 - h, ways[d]))

    def last_in(h, o):
        slot = col_at(h, OFFSETS[o], 2)
        for d in (0, 1):
            on = x_all.at[slot, quarter_of(h, d), :]
            arrived(on, last_send.at[h, o, d], last_recv.at[h, o, d], xy_device(1 - h, ways[d]))

    def add_block(step, turn):
        which = lax.rem(core + lax.div(turn, 2), 2)
        way = 1 - 2 * lax.rem(turn, 2)
        slot = slot_at(lax.rem(z - way * step + RING, RING), which)
        ratio = half // tokens * 2
        start = pl.multiple_of(lax.rem(slot, ratio) * tokens, tokens)
        left = x_all[lax.div(slot, ratio), pl.ds(start, tokens), :]
        out_ref[...] += lax.dot_general(
            left, g_all[slot], (((0,), (0,)), ((), ())), preferred_element_type=jnp.float32
        )

    def add_steps(low_step, high_step):
        def body(j, carry):
            add_block(lax.div(j, 4), lax.rem(j, 4))
            return carry

        lax.fori_loop(4 * low_step, 4 * high_step, body, 0)

    def add_pair(step):
        def body(j, carry):
            add_block(step, 2 * j)
            return carry

        lax.fori_loop(0, 2, body, 0)

    mine = slot_at(z, core)
    theirs = slot_at(z, 1 - core)
    for k in range(PARTS):
        for d in (0, 1):
            ring_start(1, d, k, g_ref.at[part(k), :], mine)
    for h in (0, 1):
        for d in (0, 1):
            along_first(h, d)
    for h in (0, 1):
        along_second(h, 0)
    send(g_ref, g_all.at[mine], core_send.at[0, FAR, 0], core_recv.at[0, FAR, 0], twin)
    own_g = pltpu.make_async_copy(g_ref, g_all.at[mine], local_sem.at[0])
    own_x = pltpu.make_async_copy(x_ref, x_all.at[col], local_sem.at[1])
    own_g.start()
    own_x.start()
    out_ref[...] = jnp.zeros_like(out_ref)

    for h in (0, 1):
        for d in (0, 1):
            first_in(h, d)
    ring_step(1)
    for h in (0, 1):
        hop_in(h)
    for h in (0, 1):
        second_in(h, 0)
    ring_step(2)
    for o in (1, 2, 3):
        for h in (0, 1):
            second_in(h, o)
    ring_step(3)
    for o in (0, 1, 2, 3):
        for h in (0, 1):
            last_in(h, o)
    own_g.wait()
    own_x.wait()
    arrived(g_all.at[theirs], core_send.at[0, FAR, 0], core_recv.at[0, FAR, 0], twin)
    for step in (1, 2):
        core_step(step)
    ring_step(4)
    add_pair(0)
    add_steps(1, 2)
    core_step(3)
    ring_step(5)
    add_steps(2, 4)
    core_step(4)
    core_step(5)
    ring_step(6)
    add_steps(4, 6)
    core_step(6)
    ring_step(7)
    add_steps(6, 7)
    core_step(7)
    ring_step(FAR)
    add_steps(7, 8)
    core_step(FAR)
    add_pair(FAR)
    for copy in sent:
        copy.wait_send()


def gathered_grad(layer_inputs, output_grads):
    rows, features = layer_inputs.shape
    tokens, units = output_grads.shape
    dma = pltpu.SemaphoreType.DMA
    return pl.pallas_call(
        grad_kernel,
        out_shape=jax.ShapeDtypeStruct((features, units), jnp.float32),
        in_specs=[pl.BlockSpec(memory_space=pl.ANY)] * 2,
        out_specs=pl.BlockSpec(memory_space=pltpu.VMEM),
        scratch_shapes=[
            pltpu.VMEM((SIDE * SIDE, rows, features), jnp.bfloat16),
            pltpu.VMEM((2 * RING, tokens, units), jnp.bfloat16),
            dma((2, FAR, PARTS)),
            dma((2, FAR, PARTS)),
            dma((2, FAR + 1, PARTS)),
            dma((2, FAR + 1, PARTS)),
            dma((2, 2)),
            dma((2, 2)),
            dma((2, 2)),
            dma((2, 2)),
            dma((2, SIDE, 2)),
            dma((2, SIDE, 2)),
            dma((2, SIDE, 2)),
            dma((2, SIDE, 2)),
            dma((2,)),
        ],
        compiler_params=pltpu.CompilerParams(
            collective_id=0, has_side_effects=True, vmem_limit_bytes=32 * 1024 * 1024
        ),
        name="gather_grad",
    )(layer_inputs, output_grads)


def per_device(layer_inputs, output_grads, weight, moment, variance, keep_mask):
    fsdp_count = lax.axis_size("fsdp")
    rank_row = lax.axis_index("row")
    rank_col = lax.axis_index("col")
    rank_fsdp = lax.axis_index("fsdp")
    row_blocks = weight.shape[0] // BS
    col_blocks = weight.shape[1] // BS
    tile_keep = lax.dynamic_slice(
        keep_mask,
        ((rank_row * fsdp_count + rank_fsdp) * row_blocks, rank_col * col_blocks),
        (row_blocks, col_blocks),
    )
    grad = gathered_grad(layer_inputs, output_grads)
    keep_elem = expand_keep(tile_keep)
    return adam_update(grad, weight, moment, variance, keep_elem)


def solution(mesh):
    placed = (
        P("col", ("row", "fsdp")),
        P(("row", "fsdp"), "col"),
        P(("row", "fsdp"), "col"),
        P(("row", "fsdp"), "col"),
        P(("row", "fsdp"), "col"),
        P(),
    )
    return jax.shard_map(
        per_device,
        mesh=mesh,
        in_specs=placed,
        out_specs=(P(("row", "fsdp"), "col"), P(("row", "fsdp"), "col"), P(("row", "fsdp"), "col")),
        check_vma=False,
    )
```

```python
import jax
import jax.numpy as jnp
from jax import lax
from jax.experimental import pallas as pl
from jax.experimental.pallas import tpu as pltpu
from jax.sharding import PartitionSpec as P

BS = 128
MESH = pl.DeviceIdType.MESH

learn_rate = 0.02
beta_one = 0.9
beta_two = 0.95
epsilon = 1e-08
decay_rate = 0.1
first_fix = 1.0 - 0.9**10
second_fix = 1.0 - 0.95**10

SIDE = 4
RING = 16
FAR = RING // 2
LOW = 4
PARTS = 2
OFFSETS = (0, 3, 1, 2)


ROWS = 64


def adam_kernel(grad_ref, keep_ref, weight_ref, moment_ref, variance_ref, *rest):
    outs, helds, sems = rest[:3], rest[3:6], rest[6]
    copies = []
    for step in range(grad_ref.shape[0] // ROWS):
        rows = pl.ds(step * ROWS, ROWS)
        block = step * ROWS // BS
        for c in range(grad_ref.shape[1] // BS):
            cols = pl.ds(c * BS, BS)
            keep = jnp.broadcast_to(keep_ref[pl.ds(block, 1), cols], (ROWS, BS)) > 0.5
            grad = grad_ref[rows, cols]
            old = [ref[rows, cols].astype(jnp.float32) for ref in (weight_ref, moment_ref, variance_ref)]
            weight, moment, variance = old
            first = beta_one * moment + (1.0 - beta_one) * grad
            second = beta_two * variance + (1.0 - beta_two) * grad * grad
            scale = first_fix * (jnp.sqrt(second * (1.0 / second_fix)) + epsilon)
            direction = first / scale + decay_rate * weight
            for held, new, kept in zip(helds, (weight - learn_rate * direction, first, second), old):
                held[rows, cols] = jnp.where(keep, new, kept).astype(held.dtype)
        for n, (held, out) in enumerate(zip(helds, outs)):
            copies.append(pltpu.make_async_copy(held.at[rows, :], out.at[rows, :], sems.at[n, step]))
            copies[-1].start()
    for copy in copies:
        copy.wait()


def adam_update(grad, keep, weight, moment, variance):
    shape = jax.ShapeDtypeStruct(weight.shape, weight.dtype)
    return pl.pallas_call(
        adam_kernel,
        out_shape=(shape,) * 3,
        in_specs=[pl.BlockSpec(memory_space=pltpu.VMEM)] * 5,
        out_specs=(pl.BlockSpec(memory_space=pltpu.HBM),) * 3,
        scratch_shapes=[pltpu.VMEM(weight.shape, weight.dtype)] * 3
        + [pltpu.SemaphoreType.DMA((3, weight.shape[0] // ROWS))],
        compiler_params=pltpu.CompilerParams(vmem_limit_bytes=16 * 1024 * 1024),
        name="adam",
    )(grad, keep, weight, moment, variance)


def grad_kernel(
    x_ref,
    g_ref,
    mask_ref,
    weight_ref,
    moment_ref,
    variance_ref,
    out_ref,
    keep_ref,
    weight_near,
    moment_near,
    variance_near,
    x_all,
    g_all,
    mask,
    ring_send,
    ring_recv,
    core_send,
    core_recv,
    first_send,
    first_recv,
    hop_send,
    hop_recv,
    second_send,
    second_recv,
    last_send,
    last_recv,
    local_sem,
):
    row = lax.axis_index("row")
    col = lax.axis_index("col")
    low = lax.axis_index("fsdp")
    core = lax.rem(row, 2)
    z = lax.div(row, 2) * LOW + low
    place = (lax.div(col, SIDE), lax.rem(col, SIDE))

    def row_at(level, which):
        return lax.div(level, LOW) * 2 + which

    def slot_at(level, which):
        return row_at(level, which) * LOW + lax.rem(level, LOW)

    def z_device(step):
        level = lax.rem(z + step + RING, RING)
        return {"row": row_at(level, core), "fsdp": lax.rem(level, LOW)}

    def col_at(axis, along, across):
        moved = lax.rem(place[axis] + along + SIDE, SIDE)
        other = lax.rem(place[1 - axis] + across + SIDE, SIDE)
        return moved * SIDE + other if axis == 0 else other * SIDE + moved

    def xy_device(axis, step):
        return {"col": col_at(axis, step, 0)}

    twin = {"row": row + 1 - 2 * core}
    ways = (1, -1)

    neighbours = [z_device(1), z_device(-1), twin]
    neighbours += [xy_device(axis, way) for axis in (0, 1) for way in ways]
    barrier = pltpu.get_barrier_semaphore()
    for device in neighbours:
        pl.semaphore_signal(barrier, inc=1, device_id=device, device_id_type=MESH)
    pl.semaphore_wait(barrier, len(neighbours))

    sent = []

    def send(src, dst, send_sem, recv_sem, device):
        copy = pltpu.make_async_remote_copy(
            src_ref=src,
            dst_ref=dst,
            send_sem=send_sem,
            recv_sem=recv_sem,
            device_id=device,
            device_id_type=MESH,
        )
        copy.start()
        sent.append(copy)

    def arrived(dst, send_sem, recv_sem, device):
        pltpu.make_async_remote_copy(
            src_ref=dst,
            dst_ref=dst,
            send_sem=send_sem,
            recv_sem=recv_sem,
            device_id=device,
            device_id_type=MESH,
        ).wait_recv()

    tokens = g_ref.shape[0]
    piece = tokens // PARTS

    def part(k):
        return pl.ds(k * piece, piece)

    def goes(step, d, k):
        return step < FAR or (step == FAR and (k < PARTS // 2) == (d == 0))

    def ring_start(step, d, k, src, slot):
        send(
            src,
            g_all.at[slot, part(k), :],
            ring_send.at[d, step - 1, k],
            ring_recv.at[d, step - 1, k],
            z_device(ways[d]),
        )

    def ring_step(step):
        for k in range(PARTS):
            for d in (0, 1):
                if not goes(step, d, k):
                    continue
                slot = slot_at(lax.rem(z - ways[d] * step + RING, RING), core)
                here = g_all.at[slot, part(k), :]
                sems = (ring_send.at[d, step - 1, k], ring_recv.at[d, step - 1, k])
                arrived(here, *sems, z_device(ways[d]))
                if goes(step + 1, d, k):
                    ring_start(step + 1, d, k, here, slot)
                send(here, here, core_send.at[d, step - 1, k], core_recv.at[d, step - 1, k], twin)

    def core_step(step):
        for k in range(PARTS):
            for d in (0, 1):
                if not goes(step, d, k):
                    continue
                slot = slot_at(lax.rem(z - ways[d] * step + RING, RING), 1 - core)
                arrived(
                    g_all.at[slot, part(k), :],
                    core_send.at[d, step - 1, k],
                    core_recv.at[d, step - 1, k],
                    twin,
                )

    half = x_ref.shape[0] // 2
    quarter = half // 2

    def half_of(h):
        return pl.ds(h * half, half)

    def quarter_of(h, d):
        return pl.ds(h * half + d * quarter, quarter)

    def along_first(h, d):
        src = x_ref.at[half_of(h), :]
        dst = x_all.at[col, half_of(h), :]
        send(src, dst, first_send.at[h, d], first_recv.at[h, d], xy_device(h, ways[d]))

    def along_second(h, o):
        slot = col_at(h, OFFSETS[o], 0)
        here = x_all.at[slot, half_of(h), :]
        src = x_ref.at[half_of(h), :] if o == 0 else here
        for d in (0, 1):
            send(src, here, second_send.at[h, o, d], second_recv.at[h, o, d], xy_device(1 - h, ways[d]))

    def first_in(h, d):
        slot = col_at(h, -ways[d], 0)
        arrived(x_all.at[slot, half_of(h), :], first_send.at[h, d], first_recv.at[h, d], xy_device(h, ways[d]))
        on = x_all.at[slot, quarter_of(h, d), :]
        send(on, on, hop_send.at[h, d], hop_recv.at[h, d], xy_device(h, ways[d]))
        along_second(h, 1 + d)

    def hop_in(h):
        slot = col_at(h, 2, 0)
        for d in (0, 1):
            on = x_all.at[slot, quarter_of(h, d), :]
            arrived(on, hop_send.at[h, d], hop_recv.at[h, d], xy_device(h, ways[d]))
        along_second(h, 3)

    def second_in(h, o):
        for d in (0, 1):
            slot = col_at(h, OFFSETS[o], -ways[d])
            sems = (second_send.at[h, o, d], second_recv.at[h, o, d])
            arrived(x_all.at[slot, half_of(h), :], *sems, xy_device(1 - h, ways[d]))
            on = x_all.at[slot, quarter_of(h, d), :]
            send(on, on, last_send.at[h, o, d], last_recv.at[h, o, d], xy_device(1 - h, ways[d]))

    def last_in(h, o):
        slot = col_at(h, OFFSETS[o], 2)
        for d in (0, 1):
            on = x_all.at[slot, quarter_of(h, d), :]
            arrived(on, last_send.at[h, o, d], last_recv.at[h, o, d], xy_device(1 - h, ways[d]))

    def add_block(step, turn):
        which = lax.rem(core + lax.div(turn, 2), 2)
        way = 1 - 2 * lax.rem(turn, 2)
        slot = slot_at(lax.rem(z - way * step + RING, RING), which)
        ratio = half // tokens * 2
        start = pl.multiple_of(lax.rem(slot, ratio) * tokens, tokens)
        left = x_all[lax.div(slot, ratio), pl.ds(start, tokens), :]
        out_ref[...] += lax.dot_general(
            left, g_all[slot], (((0,), (0,)), ((), ())), preferred_element_type=jnp.float32
        )

    def add_steps(low_step, high_step):
        def body(j, carry):
            add_block(lax.div(j, 4), lax.rem(j, 4))
            return carry

        lax.fori_loop(4 * low_step, 4 * high_step, body, 0)

    def add_one(step, which):
        def body(j, carry):
            add_block(step, 2 * j)
            return carry

        lax.fori_loop(which, which + 1, body, 0)

    def expand_keep():
        block_rows, block_cols = mask.shape
        count = out_ref.shape[0] // BS
        spread = keep_ref.shape
        top = (row * LOW + low) * count
        edge = col * (spread[1] // BS)
        pick = lax.broadcasted_iota(jnp.int32, (spread[0], block_rows), 0) + top
        pick = pick == lax.broadcasted_iota(jnp.int32, (spread[0], block_rows), 1)
        lanes = lax.broadcasted_iota(jnp.int32, (block_cols, spread[1]), 1)
        lanes = lax.shift_right_logical(lanes, 7) + edge
        lanes = lanes == lax.broadcasted_iota(jnp.int32, (block_cols, spread[1]), 0)
        kept = (mask[...] > 0).astype(jnp.float32)
        kept = jnp.dot(pick.astype(jnp.float32), kept, preferred_element_type=jnp.float32)
        keep_ref[...] = jnp.dot(kept, lanes.astype(jnp.float32), preferred_element_type=jnp.float32)

    mine = slot_at(z, core)
    theirs = slot_at(z, 1 - core)
    for k in range(PARTS):
        for d in (0, 1):
            ring_start(1, d, k, g_ref.at[part(k), :], mine)
    for h in (0, 1):
        for d in (0, 1):
            along_first(h, d)
    for h in (0, 1):
        along_second(h, 0)
    send(g_ref, g_all.at[mine], core_send.at[0, FAR, 0], core_recv.at[0, FAR, 0], twin)
    own_g = pltpu.make_async_copy(g_ref, g_all.at[mine], local_sem.at[0])
    own_x = pltpu.make_async_copy(x_ref, x_all.at[col], local_sem.at[1])
    own_mask = pltpu.make_async_copy(mask_ref, mask, local_sem.at[2])
    own_g.start()
    own_x.start()
    own_mask.start()
    out_ref[...] = jnp.zeros_like(out_ref)

    for h in (0, 1):
        for d in (0, 1):
            first_in(h, d)
    ring_step(1)
    for h in (0, 1):
        hop_in(h)
    for h in (0, 1):
        second_in(h, 0)
    ring_step(2)
    for o in (1, 2, 3):
        for h in (0, 1):
            second_in(h, o)
    ring_step(3)
    for o in (0, 1, 2, 3):
        for h in (0, 1):
            last_in(h, o)
    own_g.wait()
    own_x.wait()
    own_mask.wait()
    expand_keep()
    states = zip((weight_ref, moment_ref, variance_ref), (weight_near, moment_near, variance_near))
    loads = [
        pltpu.make_async_copy(far, near, local_sem.at[3 + n]) for n, (far, near) in enumerate(states)
    ]
    for load in loads:
        load.start()
    arrived(g_all.at[theirs], core_send.at[0, FAR, 0], core_recv.at[0, FAR, 0], twin)
    for step in (1, 2):
        core_step(step)
    ring_step(4)
    add_one(0, 0)
    add_one(0, 1)
    add_steps(1, 2)
    core_step(3)
    ring_step(5)
    add_steps(2, 4)
    core_step(4)
    core_step(5)
    ring_step(6)
    add_steps(4, 6)
    core_step(6)
    ring_step(7)
    add_steps(6, 7)
    core_step(7)
    add_steps(7, 8)
    ring_step(FAR)
    add_one(FAR, 0)
    core_step(FAR)
    add_one(FAR, 1)
    for load in loads:
        load.wait()
    for copy in sent:
        copy.wait_send()


def gathered_grad(layer_inputs, output_grads, keep_mask, *states):
    rows, features = layer_inputs.shape
    tokens, units = output_grads.shape
    dma = pltpu.SemaphoreType.DMA
    operands = [
        pltpu.with_memory_space_constraint(array, pltpu.HBM)
        for array in (layer_inputs, output_grads, keep_mask, *states)
    ]
    return pl.pallas_call(
        grad_kernel,
        out_shape=(
            jax.ShapeDtypeStruct((features, units), jnp.float32),
            jax.ShapeDtypeStruct((8, units), jnp.float32),
            *(jax.ShapeDtypeStruct(state.shape, state.dtype) for state in states),
        ),
        in_specs=[pl.BlockSpec(memory_space=pltpu.HBM)] * 6,
        out_specs=(pl.BlockSpec(memory_space=pltpu.VMEM),) * 5,
        scratch_shapes=[
            pltpu.VMEM((SIDE * SIDE, rows, features), jnp.bfloat16),
            pltpu.VMEM((2 * RING, tokens, units), jnp.bfloat16),
            pltpu.VMEM(keep_mask.shape, jnp.int32),
            dma((2, FAR, PARTS)),
            dma((2, FAR, PARTS)),
            dma((2, FAR + 1, PARTS)),
            dma((2, FAR + 1, PARTS)),
            dma((2, 2)),
            dma((2, 2)),
            dma((2, 2)),
            dma((2, 2)),
            dma((2, SIDE, 2)),
            dma((2, SIDE, 2)),
            dma((2, SIDE, 2)),
            dma((2, SIDE, 2)),
            dma((6,)),
        ],
        compiler_params=pltpu.CompilerParams(
            collective_id=0, has_side_effects=True, vmem_limit_bytes=32 * 1024 * 1024
        ),
        name="gather_grad",
    )(*operands)


def per_device(layer_inputs, output_grads, weight, moment, variance, keep_mask):
    near = gathered_grad(layer_inputs, output_grads, keep_mask, weight, moment, variance)
    return adam_update(*near)


def solution(mesh):
    placed = (
        P("col", ("row", "fsdp")),
        P(("row", "fsdp"), "col"),
        P(("row", "fsdp"), "col"),
        P(("row", "fsdp"), "col"),
        P(("row", "fsdp"), "col"),
        P(),
    )
    return jax.shard_map(
        per_device,
        mesh=mesh,
        in_specs=placed,
        out_specs=(P(("row", "fsdp"), "col"), P(("row", "fsdp"), "col"), P(("row", "fsdp"), "col")),
        check_vma=False,
    )
```

```python
import jax
import jax.numpy as jnp
from jax import lax
from jax.experimental import pallas as pl
from jax.experimental.pallas import tpu as pltpu
from jax.sharding import PartitionSpec as P

BS = 128
MESH = pl.DeviceIdType.MESH

learn_rate = 0.02
beta_one = 0.9
beta_two = 0.95
epsilon = 1e-08
decay_rate = 0.1
first_fix = 1.0 - 0.9**10
second_fix = 1.0 - 0.95**10

SIDE = 4
RING = 16
FAR = RING // 2
LOW = 4
PARTS = 2
OFFSETS = (0, 3, 1, 2)


ROWS = 64


def adam_kernel(grad_ref, keep_ref, weight_ref, moment_ref, variance_ref, *rest):
    outs, helds, sems = rest[:3], rest[3:6], rest[6]
    copies = []
    for step in range(grad_ref.shape[0] // ROWS):
        rows = pl.ds(step * ROWS, ROWS)
        block = step * ROWS // BS
        for c in range(grad_ref.shape[1] // BS):
            cols = pl.ds(c * BS, BS)
            keep = jnp.broadcast_to(keep_ref[pl.ds(block, 1), cols], (ROWS, BS)) > 0.5
            grad = grad_ref[rows, cols]
            old = [ref[rows, cols].astype(jnp.float32) for ref in (weight_ref, moment_ref, variance_ref)]
            weight, moment, variance = old
            first = beta_one * moment + (1.0 - beta_one) * grad
            second = beta_two * variance + (1.0 - beta_two) * grad * grad
            scale = first_fix * (jnp.sqrt(second * (1.0 / second_fix)) + epsilon)
            direction = first / scale + decay_rate * weight
            for held, new, kept in zip(helds, (weight - learn_rate * direction, first, second), old):
                held[rows, cols] = jnp.where(keep, new, kept).astype(held.dtype)
        for n, (held, out) in enumerate(zip(helds, outs)):
            copies.append(pltpu.make_async_copy(held.at[rows, :], out.at[rows, :], sems.at[n, step]))
            copies[-1].start()
    for copy in copies:
        copy.wait()


def adam_update(grad, keep, weight, moment, variance):
    shape = jax.ShapeDtypeStruct(weight.shape, weight.dtype)
    return pl.pallas_call(
        adam_kernel,
        out_shape=(shape,) * 3,
        in_specs=[pl.BlockSpec(memory_space=pltpu.VMEM)] * 5,
        out_specs=(pl.BlockSpec(memory_space=pltpu.HBM),) * 3,
        scratch_shapes=[pltpu.VMEM(weight.shape, weight.dtype)] * 3
        + [pltpu.SemaphoreType.DMA((3, weight.shape[0] // ROWS))],
        compiler_params=pltpu.CompilerParams(vmem_limit_bytes=16 * 1024 * 1024),
        name="adam",
    )(grad, keep, weight, moment, variance)


def grad_kernel(
    x_ref,
    g_ref,
    mask_ref,
    weight_ref,
    moment_ref,
    variance_ref,
    out_ref,
    keep_ref,
    weight_near,
    moment_near,
    variance_near,
    x_all,
    g_all,
    mask,
    ring_send,
    ring_recv,
    core_send,
    core_recv,
    first_send,
    first_recv,
    hop_send,
    hop_recv,
    second_send,
    second_recv,
    last_send,
    last_recv,
    local_sem,
):
    row = lax.axis_index("row")
    col = lax.axis_index("col")
    low = lax.axis_index("fsdp")
    core = lax.rem(row, 2)
    z = lax.div(row, 2) * LOW + low
    place = (lax.div(col, SIDE), lax.rem(col, SIDE))

    def row_at(level, which):
        return lax.div(level, LOW) * 2 + which

    def slot_at(level, which):
        return row_at(level, which) * LOW + lax.rem(level, LOW)

    def z_device(step):
        level = lax.rem(z + step + RING, RING)
        return {"row": row_at(level, core), "fsdp": lax.rem(level, LOW)}

    def col_at(axis, along, across):
        moved = lax.rem(place[axis] + along + SIDE, SIDE)
        other = lax.rem(place[1 - axis] + across + SIDE, SIDE)
        return moved * SIDE + other if axis == 0 else other * SIDE + moved

    def xy_device(axis, step):
        return {"col": col_at(axis, step, 0)}

    twin = {"row": row + 1 - 2 * core}
    ways = (1, -1)

    neighbours = [z_device(1), z_device(-1), twin]
    neighbours += [xy_device(axis, way) for axis in (0, 1) for way in ways]
    barrier = pltpu.get_barrier_semaphore()
    for device in neighbours:
        pl.semaphore_signal(barrier, inc=1, device_id=device, device_id_type=MESH)
    pl.semaphore_wait(barrier, len(neighbours))

    sent = []

    def send(src, dst, send_sem, recv_sem, device):
        copy = pltpu.make_async_remote_copy(
            src_ref=src,
            dst_ref=dst,
            send_sem=send_sem,
            recv_sem=recv_sem,
            device_id=device,
            device_id_type=MESH,
        )
        copy.start()
        sent.append(copy)

    def arrived(dst, send_sem, recv_sem, device):
        pltpu.make_async_remote_copy(
            src_ref=dst,
            dst_ref=dst,
            send_sem=send_sem,
            recv_sem=recv_sem,
            device_id=device,
            device_id_type=MESH,
        ).wait_recv()

    tokens = g_ref.shape[0]
    piece = tokens // PARTS

    def part(k):
        return pl.ds(k * piece, piece)

    order = [(d, (i, PARTS - 1 - i)[d]) for i in range(PARTS) for d in (0, 1)]

    def goes(step, d, k):
        return step < FAR or (step == FAR and (k < PARTS // 2) == (d == 0))

    def ring_start(step, d, k, src, slot):
        send(
            src,
            g_all.at[slot, part(k), :],
            ring_send.at[d, step - 1, k],
            ring_recv.at[d, step - 1, k],
            z_device(ways[d]),
        )

    def ring_step(step):
        for d, k in order:
            if not goes(step, d, k):
                continue
            slot = slot_at(lax.rem(z - ways[d] * step + RING, RING), core)
            here = g_all.at[slot, part(k), :]
            sems = (ring_send.at[d, step - 1, k], ring_recv.at[d, step - 1, k])
            arrived(here, *sems, z_device(ways[d]))
            if goes(step + 1, d, k):
                ring_start(step + 1, d, k, here, slot)
            send(here, here, core_send.at[d, step - 1, k], core_recv.at[d, step - 1, k], twin)

    def core_step(step):
        for d, k in order:
            if not goes(step, d, k):
                continue
            slot = slot_at(lax.rem(z - ways[d] * step + RING, RING), 1 - core)
            arrived(
                g_all.at[slot, part(k), :],
                core_send.at[d, step - 1, k],
                core_recv.at[d, step - 1, k],
                twin,
            )

    half = x_ref.shape[0] // 2
    quarter = half // 2

    def half_of(h):
        return pl.ds(h * half, half)

    def quarter_of(h, d):
        return pl.ds(h * half + d * quarter, quarter)

    def along_first(h, d):
        src = x_ref.at[half_of(h), :]
        dst = x_all.at[col, half_of(h), :]
        send(src, dst, first_send.at[h, d], first_recv.at[h, d], xy_device(h, ways[d]))

    def along_second(h, o):
        slot = col_at(h, OFFSETS[o], 0)
        here = x_all.at[slot, half_of(h), :]
        src = x_ref.at[half_of(h), :] if o == 0 else here
        for d in (0, 1):
            send(src, here, second_send.at[h, o, d], second_recv.at[h, o, d], xy_device(1 - h, ways[d]))

    def first_in(h, d):
        slot = col_at(h, -ways[d], 0)
        arrived(x_all.at[slot, half_of(h), :], first_send.at[h, d], first_recv.at[h, d], xy_device(h, ways[d]))
        on = x_all.at[slot, quarter_of(h, d), :]
        send(on, on, hop_send.at[h, d], hop_recv.at[h, d], xy_device(h, ways[d]))
        along_second(h, 1 + d)

    def hop_in(h):
        slot = col_at(h, 2, 0)
        for d in (0, 1):
            on = x_all.at[slot, quarter_of(h, d), :]
            arrived(on, hop_send.at[h, d], hop_recv.at[h, d], xy_device(h, ways[d]))
        along_second(h, 3)

    def second_in(h, o):
        for d in (0, 1):
            slot = col_at(h, OFFSETS[o], -ways[d])
            sems = (second_send.at[h, o, d], second_recv.at[h, o, d])
            arrived(x_all.at[slot, half_of(h), :], *sems, xy_device(1 - h, ways[d]))
            on = x_all.at[slot, quarter_of(h, d), :]
            send(on, on, last_send.at[h, o, d], last_recv.at[h, o, d], xy_device(1 - h, ways[d]))

    def last_in(h, o):
        slot = col_at(h, OFFSETS[o], 2)
        for d in (0, 1):
            on = x_all.at[slot, quarter_of(h, d), :]
            arrived(on, last_send.at[h, o, d], last_recv.at[h, o, d], xy_device(1 - h, ways[d]))

    def add_block(step, turn):
        which = lax.rem(core + lax.div(turn, 2), 2)
        way = 1 - 2 * lax.rem(turn, 2)
        slot = slot_at(lax.rem(z - way * step + RING, RING), which)
        ratio = half // tokens * 2
        start = pl.multiple_of(lax.rem(slot, ratio) * tokens, tokens)
        left = x_all[lax.div(slot, ratio), pl.ds(start, tokens), :]
        out_ref[...] += lax.dot_general(
            left, g_all[slot], (((0,), (0,)), ((), ())), preferred_element_type=jnp.float32
        )

    def add_steps(low_step, high_step):
        def body(j, carry):
            add_block(lax.div(j, 4), lax.rem(j, 4))
            return carry

        lax.fori_loop(4 * low_step, 4 * high_step, body, 0)

    def add_turns(step, begin, end):
        def body(j, carry):
            add_block(step, j)
            return carry

        lax.fori_loop(begin, end, body, 0)

    def add_one(step, which):
        def body(j, carry):
            add_block(step, 2 * j)
            return carry

        lax.fori_loop(which, which + 1, body, 0)

    def expand_keep():
        block_rows, block_cols = mask.shape
        count = out_ref.shape[0] // BS
        spread = keep_ref.shape
        top = (row * LOW + low) * count
        edge = col * (spread[1] // BS)
        pick = lax.broadcasted_iota(jnp.int32, (spread[0], block_rows), 0) + top
        pick = pick == lax.broadcasted_iota(jnp.int32, (spread[0], block_rows), 1)
        lanes = lax.broadcasted_iota(jnp.int32, (block_cols, spread[1]), 1)
        lanes = lax.shift_right_logical(lanes, 7) + edge
        lanes = lanes == lax.broadcasted_iota(jnp.int32, (block_cols, spread[1]), 0)
        kept = (mask[...] > 0).astype(jnp.float32)
        kept = jnp.dot(pick.astype(jnp.float32), kept, preferred_element_type=jnp.float32)
        keep_ref[...] = jnp.dot(kept, lanes.astype(jnp.float32), preferred_element_type=jnp.float32)

    mine = slot_at(z, core)
    theirs = slot_at(z, 1 - core)
    for d, k in order:
        ring_start(1, d, k, g_ref.at[part(k), :], mine)
    for h in (0, 1):
        for d in (0, 1):
            along_first(h, d)
    for h in (0, 1):
        along_second(h, 0)
    send(g_ref, g_all.at[mine], core_send.at[0, FAR, 0], core_recv.at[0, FAR, 0], twin)
    own_g = pltpu.make_async_copy(g_ref, g_all.at[mine], local_sem.at[0])
    own_x = pltpu.make_async_copy(x_ref, x_all.at[col], local_sem.at[1])
    own_mask = pltpu.make_async_copy(mask_ref, mask, local_sem.at[2])
    own_g.start()
    own_x.start()
    own_mask.start()
    out_ref[...] = jnp.zeros_like(out_ref)

    for h in (0, 1):
        for d in (0, 1):
            first_in(h, d)
    ring_step(1)
    for h in (0, 1):
        hop_in(h)
    for h in (0, 1):
        second_in(h, 0)
    ring_step(2)
    for o in (1, 2, 3):
        for h in (0, 1):
            second_in(h, o)
    ring_step(3)
    for o in (0, 1, 2, 3):
        for h in (0, 1):
            last_in(h, o)
    own_g.wait()
    own_x.wait()
    own_mask.wait()
    expand_keep()
    states = zip((weight_ref, moment_ref, variance_ref), (weight_near, moment_near, variance_near))
    loads = [
        pltpu.make_async_copy(far, near, local_sem.at[3 + n]) for n, (far, near) in enumerate(states)
    ]
    for load in loads:
        load.start()
    arrived(g_all.at[theirs], core_send.at[0, FAR, 0], core_recv.at[0, FAR, 0], twin)
    for step in (1, 2):
        core_step(step)
    ring_step(4)
    add_one(0, 0)
    add_one(0, 1)
    add_steps(1, 2)
    core_step(3)
    ring_step(5)
    add_steps(2, 4)
    core_step(4)
    core_step(5)
    ring_step(6)
    add_steps(4, 6)
    core_step(6)
    ring_step(7)
    add_steps(6, 7)
    add_turns(7, 0, 2)
    ring_step(FAR)
    core_step(7)
    add_turns(7, 2, 4)
    add_one(FAR, 0)
    core_step(FAR)
    add_one(FAR, 1)
    for load in loads:
        load.wait()
    for copy in sent:
        copy.wait_send()


def gathered_grad(layer_inputs, output_grads, keep_mask, *states):
    rows, features = layer_inputs.shape
    tokens, units = output_grads.shape
    dma = pltpu.SemaphoreType.DMA
    operands = [
        pltpu.with_memory_space_constraint(array, pltpu.HBM)
        for array in (layer_inputs, output_grads, keep_mask, *states)
    ]
    return pl.pallas_call(
        grad_kernel,
        out_shape=(
            jax.ShapeDtypeStruct((features, units), jnp.float32),
            jax.ShapeDtypeStruct((8, units), jnp.float32),
            *(jax.ShapeDtypeStruct(state.shape, state.dtype) for state in states),
        ),
        in_specs=[pl.BlockSpec(memory_space=pltpu.HBM)] * 6,
        out_specs=(pl.BlockSpec(memory_space=pltpu.VMEM),) * 5,
        scratch_shapes=[
            pltpu.VMEM((SIDE * SIDE, rows, features), jnp.bfloat16),
            pltpu.VMEM((2 * RING, tokens, units), jnp.bfloat16),
            pltpu.VMEM(keep_mask.shape, jnp.int32),
            dma((2, FAR, PARTS)),
            dma((2, FAR, PARTS)),
            dma((2, FAR + 1, PARTS)),
            dma((2, FAR + 1, PARTS)),
            dma((2, 2)),
            dma((2, 2)),
            dma((2, 2)),
            dma((2, 2)),
            dma((2, SIDE, 2)),
            dma((2, SIDE, 2)),
            dma((2, SIDE, 2)),
            dma((2, SIDE, 2)),
            dma((6,)),
        ],
        compiler_params=pltpu.CompilerParams(
            collective_id=0, has_side_effects=True, vmem_limit_bytes=32 * 1024 * 1024
        ),
        name="gather_grad",
    )(*operands)


def per_device(layer_inputs, output_grads, weight, moment, variance, keep_mask):
    near = gathered_grad(layer_inputs, output_grads, keep_mask, weight, moment, variance)
    return adam_update(*near)


def solution(mesh):
    placed = (
        P("col", ("row", "fsdp")),
        P(("row", "fsdp"), "col"),
        P(("row", "fsdp"), "col"),
        P(("row", "fsdp"), "col"),
        P(("row", "fsdp"), "col"),
        P(),
    )
    return jax.shard_map(
        per_device,
        mesh=mesh,
        in_specs=placed,
        out_specs=(P(("row", "fsdp"), "col"), P(("row", "fsdp"), "col"), P(("row", "fsdp"), "col")),
        check_vma=False,
    )
```

```python
import jax
import jax.numpy as jnp
from jax import lax
from jax.experimental import pallas as pl
from jax.experimental.pallas import tpu as pltpu
from jax.sharding import PartitionSpec as P

BS = 128
MESH = pl.DeviceIdType.MESH

learn_rate = 0.02
beta_one = 0.9
beta_two = 0.95
epsilon = 1e-08
decay_rate = 0.1
first_fix = 1.0 - 0.9**10
second_fix = 1.0 - 0.95**10

shrink = 1.0 - learn_rate * decay_rate
root_scale = first_fix / learn_rate * second_fix**-0.5
root_shift = first_fix * epsilon / learn_rate

SIDE = 4
RING = 16
FAR = RING // 2
LOW = 4
PARTS = 2
OFFSETS = (0, 3, 1, 2)


ROWS = 64


def adam_kernel(grad_ref, keep_ref, weight_ref, moment_ref, variance_ref, *rest):
    outs, helds, sems = rest[:3], rest[3:6], rest[6]
    copies = []
    for step in range(grad_ref.shape[0] // ROWS):
        rows = pl.ds(step * ROWS, ROWS)
        block = step * ROWS // BS
        for c in range(grad_ref.shape[1] // BS):
            cols = pl.ds(c * BS, BS)
            keep = jnp.broadcast_to(keep_ref[pl.ds(block, 1), cols], (ROWS, BS)).astype(jnp.bfloat16) > 0.5
            grad = grad_ref[rows, cols]
            old = [ref[rows, cols] for ref in (weight_ref, moment_ref, variance_ref)]
            weight, moment, variance = [value.astype(jnp.float32) for value in old]
            first = beta_one * moment + (1.0 - beta_one) * grad
            second = beta_two * variance + (1.0 - beta_two) * grad * grad
            change = first / (jnp.sqrt(second) * root_scale + root_shift)
            for held, new, kept in zip(helds, (weight * shrink - change, first, second), old):
                held[rows, cols] = jnp.where(keep, new.astype(held.dtype), kept)
        for n, (held, out) in enumerate(zip(helds, outs)):
            copies.append(pltpu.make_async_copy(held.at[rows, :], out.at[rows, :], sems.at[n, step]))
            copies[-1].start()
    for copy in copies:
        copy.wait()


def adam_update(grad, keep, weight, moment, variance):
    shape = jax.ShapeDtypeStruct(weight.shape, weight.dtype)
    return pl.pallas_call(
        adam_kernel,
        out_shape=(shape,) * 3,
        in_specs=[pl.BlockSpec(memory_space=pltpu.VMEM)] * 5,
        out_specs=(pl.BlockSpec(memory_space=pltpu.HBM),) * 3,
        scratch_shapes=[pltpu.VMEM(weight.shape, weight.dtype)] * 3
        + [pltpu.SemaphoreType.DMA((3, weight.shape[0] // ROWS))],
        compiler_params=pltpu.CompilerParams(vmem_limit_bytes=16 * 1024 * 1024),
        name="adam",
    )(grad, keep, weight, moment, variance)


def grad_kernel(
    x_ref,
    g_ref,
    mask_ref,
    weight_ref,
    moment_ref,
    variance_ref,
    out_ref,
    keep_ref,
    weight_near,
    moment_near,
    variance_near,
    x_all,
    g_all,
    mask,
    ring_send,
    ring_recv,
    core_send,
    core_recv,
    first_send,
    first_recv,
    hop_send,
    hop_recv,
    second_send,
    second_recv,
    last_send,
    last_recv,
    local_sem,
):
    row = lax.axis_index("row")
    col = lax.axis_index("col")
    low = lax.axis_index("fsdp")
    core = lax.rem(row, 2)
    z = lax.div(row, 2) * LOW + low
    place = (lax.div(col, SIDE), lax.rem(col, SIDE))

    def row_at(level, which):
        return lax.div(level, LOW) * 2 + which

    def slot_at(level, which):
        return row_at(level, which) * LOW + lax.rem(level, LOW)

    def z_device(step):
        level = lax.rem(z + step + RING, RING)
        return {"row": row_at(level, core), "fsdp": lax.rem(level, LOW)}

    def col_at(axis, along, across):
        moved = lax.rem(place[axis] + along + SIDE, SIDE)
        other = lax.rem(place[1 - axis] + across + SIDE, SIDE)
        return moved * SIDE + other if axis == 0 else other * SIDE + moved

    def xy_device(axis, step):
        return {"col": col_at(axis, step, 0)}

    twin = {"row": row + 1 - 2 * core}
    ways = (1, -1)

    neighbours = [z_device(1), z_device(-1), twin]
    neighbours += [xy_device(axis, way) for axis in (0, 1) for way in ways]
    barrier = pltpu.get_barrier_semaphore()
    for device in neighbours:
        pl.semaphore_signal(barrier, inc=1, device_id=device, device_id_type=MESH)
    pl.semaphore_wait(barrier, len(neighbours))

    sent = []

    def send(src, dst, send_sem, recv_sem, device):
        copy = pltpu.make_async_remote_copy(
            src_ref=src,
            dst_ref=dst,
            send_sem=send_sem,
            recv_sem=recv_sem,
            device_id=device,
            device_id_type=MESH,
        )
        copy.start()
        sent.append(copy)

    def arrived(dst, send_sem, recv_sem, device):
        pltpu.make_async_remote_copy(
            src_ref=dst,
            dst_ref=dst,
            send_sem=send_sem,
            recv_sem=recv_sem,
            device_id=device,
            device_id_type=MESH,
        ).wait_recv()

    tokens = g_ref.shape[0]
    piece = tokens // PARTS

    def part(k):
        return pl.ds(k * piece, piece)

    order = [(d, (i, PARTS - 1 - i)[d]) for i in range(PARTS) for d in (0, 1)]

    def goes(step, d, k):
        return step < FAR or (step == FAR and (k < PARTS // 2) == (d == 0))

    def ring_start(step, d, k, src, slot):
        send(
            src,
            g_all.at[slot, part(k), :],
            ring_send.at[d, step - 1, k],
            ring_recv.at[d, step - 1, k],
            z_device(ways[d]),
        )

    def ring_step(step):
        for d, k in order:
            if not goes(step, d, k):
                continue
            slot = slot_at(lax.rem(z - ways[d] * step + RING, RING), core)
            here = g_all.at[slot, part(k), :]
            sems = (ring_send.at[d, step - 1, k], ring_recv.at[d, step - 1, k])
            arrived(here, *sems, z_device(ways[d]))
            if goes(step + 1, d, k):
                ring_start(step + 1, d, k, here, slot)
            send(here, here, core_send.at[d, step - 1, k], core_recv.at[d, step - 1, k], twin)

    def core_step(step):
        for d, k in order:
            if not goes(step, d, k):
                continue
            slot = slot_at(lax.rem(z - ways[d] * step + RING, RING), 1 - core)
            arrived(
                g_all.at[slot, part(k), :],
                core_send.at[d, step - 1, k],
                core_recv.at[d, step - 1, k],
                twin,
            )

    half = x_ref.shape[0] // 2
    quarter = half // 2

    def half_of(h):
        return pl.ds(h * half, half)

    def quarter_of(h, d):
        return pl.ds(h * half + d * quarter, quarter)

    def along_first(h, d):
        src = x_ref.at[half_of(h), :]
        dst = x_all.at[col, half_of(h), :]
        send(src, dst, first_send.at[h, d], first_recv.at[h, d], xy_device(h, ways[d]))

    def along_second(h, o):
        slot = col_at(h, OFFSETS[o], 0)
        here = x_all.at[slot, half_of(h), :]
        src = x_ref.at[half_of(h), :] if o == 0 else here
        for d in (0, 1):
            send(src, here, second_send.at[h, o, d], second_recv.at[h, o, d], xy_device(1 - h, ways[d]))

    def first_in(h, d):
        slot = col_at(h, -ways[d], 0)
        arrived(x_all.at[slot, half_of(h), :], first_send.at[h, d], first_recv.at[h, d], xy_device(h, ways[d]))
        on = x_all.at[slot, quarter_of(h, d), :]
        send(on, on, hop_send.at[h, d], hop_recv.at[h, d], xy_device(h, ways[d]))
        along_second(h, 1 + d)

    def hop_in(h):
        slot = col_at(h, 2, 0)
        for d in (0, 1):
            on = x_all.at[slot, quarter_of(h, d), :]
            arrived(on, hop_send.at[h, d], hop_recv.at[h, d], xy_device(h, ways[d]))
        along_second(h, 3)

    def second_in(h, o):
        for d in (0, 1):
            slot = col_at(h, OFFSETS[o], -ways[d])
            sems = (second_send.at[h, o, d], second_recv.at[h, o, d])
            arrived(x_all.at[slot, half_of(h), :], *sems, xy_device(1 - h, ways[d]))
            on = x_all.at[slot, quarter_of(h, d), :]
            send(on, on, last_send.at[h, o, d], last_recv.at[h, o, d], xy_device(1 - h, ways[d]))

    def last_in(h, o):
        slot = col_at(h, OFFSETS[o], 2)
        for d in (0, 1):
            on = x_all.at[slot, quarter_of(h, d), :]
            arrived(on, last_send.at[h, o, d], last_recv.at[h, o, d], xy_device(1 - h, ways[d]))

    def add_block(step, turn):
        which = lax.rem(core + lax.div(turn, 2), 2)
        way = 1 - 2 * lax.rem(turn, 2)
        slot = slot_at(lax.rem(z - way * step + RING, RING), which)
        ratio = half // tokens * 2
        start = pl.multiple_of(lax.rem(slot, ratio) * tokens, tokens)
        left = x_all[lax.div(slot, ratio), pl.ds(start, tokens), :]
        out_ref[...] += lax.dot_general(
            left, g_all[slot], (((0,), (0,)), ((), ())), preferred_element_type=jnp.float32
        )

    def add_steps(low_step, high_step):
        def body(j, carry):
            add_block(lax.div(j, 4), lax.rem(j, 4))
            return carry

        lax.fori_loop(4 * low_step, 4 * high_step, body, 0)

    def add_turns(step, begin, end):
        def body(j, carry):
            add_block(step, j)
            return carry

        lax.fori_loop(begin, end, body, 0)

    def add_one(step, which):
        def body(j, carry):
            add_block(step, 2 * j)
            return carry

        lax.fori_loop(which, which + 1, body, 0)

    def expand_keep():
        block_rows, block_cols = mask.shape
        count = out_ref.shape[0] // BS
        spread = keep_ref.shape
        top = (row * LOW + low) * count
        edge = col * (spread[1] // BS)
        pick = lax.broadcasted_iota(jnp.int32, (spread[0], block_rows), 0) + top
        pick = pick == lax.broadcasted_iota(jnp.int32, (spread[0], block_rows), 1)
        lanes = lax.broadcasted_iota(jnp.int32, (block_cols, spread[1]), 1)
        lanes = lax.shift_right_logical(lanes, 7) + edge
        lanes = lanes == lax.broadcasted_iota(jnp.int32, (block_cols, spread[1]), 0)
        kept = (mask[...] > 0).astype(jnp.float32)
        kept = jnp.dot(pick.astype(jnp.float32), kept, preferred_element_type=jnp.float32)
        keep_ref[...] = jnp.dot(kept, lanes.astype(jnp.float32), preferred_element_type=jnp.float32)

    mine = slot_at(z, core)
    theirs = slot_at(z, 1 - core)
    for d, k in order:
        ring_start(1, d, k, g_ref.at[part(k), :], mine)
    for h in (0, 1):
        for d in (0, 1):
            along_first(h, d)
    for h in (0, 1):
        along_second(h, 0)
    send(g_ref, g_all.at[mine], core_send.at[0, FAR, 0], core_recv.at[0, FAR, 0], twin)
    own_g = pltpu.make_async_copy(g_ref, g_all.at[mine], local_sem.at[0])
    own_x = pltpu.make_async_copy(x_ref, x_all.at[col], local_sem.at[1])
    own_mask = pltpu.make_async_copy(mask_ref, mask, local_sem.at[2])
    own_g.start()
    own_x.start()
    own_mask.start()
    out_ref[...] = jnp.zeros_like(out_ref)

    for h in (0, 1):
        for d in (0, 1):
            first_in(h, d)
    ring_step(1)
    for h in (0, 1):
        hop_in(h)
    for h in (0, 1):
        second_in(h, 0)
    ring_step(2)
    for o in (1, 2, 3):
        for h in (0, 1):
            second_in(h, o)
    ring_step(3)
    for o in (0, 1, 2, 3):
        for h in (0, 1):
            last_in(h, o)
    own_g.wait()
    own_x.wait()
    own_mask.wait()
    expand_keep()
    states = zip((weight_ref, moment_ref, variance_ref), (weight_near, moment_near, variance_near))
    loads = [
        pltpu.make_async_copy(far, near, local_sem.at[3 + n]) for n, (far, near) in enumerate(states)
    ]
    for load in loads:
        load.start()
    arrived(g_all.at[theirs], core_send.at[0, FAR, 0], core_recv.at[0, FAR, 0], twin)
    for step in (1, 2):
        core_step(step)
    ring_step(4)
    add_one(0, 0)
    add_one(0, 1)
    add_steps(1, 2)
    core_step(3)
    ring_step(5)
    add_steps(2, 4)
    core_step(4)
    core_step(5)
    ring_step(6)
    add_steps(4, 6)
    core_step(6)
    ring_step(7)
    add_steps(6, 7)
    add_turns(7, 0, 2)
    ring_step(FAR)
    core_step(7)
    add_turns(7, 2, 4)
    add_one(FAR, 0)
    core_step(FAR)
    add_one(FAR, 1)
    for load in loads:
        load.wait()
    for copy in sent:
        copy.wait_send()


def gathered_grad(layer_inputs, output_grads, keep_mask, *states):
    rows, features = layer_inputs.shape
    tokens, units = output_grads.shape
    dma = pltpu.SemaphoreType.DMA
    operands = [
        pltpu.with_memory_space_constraint(array, pltpu.HBM)
        for array in (layer_inputs, output_grads, keep_mask, *states)
    ]
    return pl.pallas_call(
        grad_kernel,
        out_shape=(
            jax.ShapeDtypeStruct((features, units), jnp.float32),
            jax.ShapeDtypeStruct((8, units), jnp.float32),
            *(jax.ShapeDtypeStruct(state.shape, state.dtype) for state in states),
        ),
        in_specs=[pl.BlockSpec(memory_space=pltpu.HBM)] * 6,
        out_specs=(pl.BlockSpec(memory_space=pltpu.VMEM),) * 5,
        scratch_shapes=[
            pltpu.VMEM((SIDE * SIDE, rows, features), jnp.bfloat16),
            pltpu.VMEM((2 * RING, tokens, units), jnp.bfloat16),
            pltpu.VMEM(keep_mask.shape, jnp.int32),
            dma((2, FAR, PARTS)),
            dma((2, FAR, PARTS)),
            dma((2, FAR + 1, PARTS)),
            dma((2, FAR + 1, PARTS)),
            dma((2, 2)),
            dma((2, 2)),
            dma((2, 2)),
            dma((2, 2)),
            dma((2, SIDE, 2)),
            dma((2, SIDE, 2)),
            dma((2, SIDE, 2)),
            dma((2, SIDE, 2)),
            dma((6,)),
        ],
        compiler_params=pltpu.CompilerParams(
            collective_id=0, has_side_effects=True, vmem_limit_bytes=32 * 1024 * 1024
        ),
        name="gather_grad",
    )(*operands)


def per_device(layer_inputs, output_grads, weight, moment, variance, keep_mask):
    near = gathered_grad(layer_inputs, output_grads, keep_mask, weight, moment, variance)
    return adam_update(*near)


def solution(mesh):
    placed = (
        P("col", ("row", "fsdp")),
        P(("row", "fsdp"), "col"),
        P(("row", "fsdp"), "col"),
        P(("row", "fsdp"), "col"),
        P(("row", "fsdp"), "col"),
        P(),
    )
    return jax.shard_map(
        per_device,
        mesh=mesh,
        in_specs=placed,
        out_specs=(P(("row", "fsdp"), "col"), P(("row", "fsdp"), "col"), P(("row", "fsdp"), "col")),
        check_vma=False,
    )
```
